32 devices in a mesh: lev: 4 (over x, core), row: 8 (over z, y).
Axes of the slice: x: 2, y: 2, z: 4, core: 2. Of those that a mesh axis runs over, the one named last changes fastest.
Arguments:
- wind_east: float32 [16, 128, 1024], P('lev', 'row'), may hold values from -3 to 3
- wind_north: float32 [16, 128, 1024], P('lev', 'row'), may hold values from -3 to 3
- thickness: float32 [16, 128, 1024], P('lev', 'row'), may hold values from 0.5 to 2
- tracer_one: float32 [16, 128, 1024], P('lev', 'row'), may hold values from 0 to 1
- tracer_two: float32 [16, 128, 1024], P('lev', 'row'), may hold values from 0.1 to 1
- theta_step: float32 [16], replicated, may hold values from 0.5 to 2
- surface_geopot: float32 [128, 1024], P('row'), may hold values from -12 to 12
- map_factor: float32 [128, 1024], P('row'), may hold values from 0.5 to 2
- active_layers: int32 [128, 1024], P('row'), may hold values from 8 to 16
Outputs:
- east_out: float32 [16, 128, 1024], P('lev', 'row')
- north_out: float32 [16, 128, 1024], P('lev', 'row')
- thickness_out: float32 [16, 128, 1024], P('lev', 'row')
- tracer_one_out: float32 [16, 128, 1024], P('lev', 'row')
- tracer_two_out: float32 [16, 128, 1024], P('lev', 'row')
The draws below stay inside these ranges and needn't reach their ends.
Inputs may be any that keep to these rules, and one draw needn't show every extreme that they name: Layers k with k >= active_layers of their column are below ground and keep their values.
All inputs are finite; a program needn't handle non-finite values.
Results may differ from the reference program's by a relative error of at most 0.00002.
Values sent between devices are 32-bit elements; how exact they have to be, the bound alone decides.
No kernel may reach another device: no remote copies, remote signals or barrier semaphores. Data moves between devices by JAX's collectives and lax.ppermute only.
A program may use at most 64 MiB of HBM per device.

```python
import math
import jax
import jax.numpy as jnp

NY = 1024
OUTER = 2
L = 16
NX = 128


def plant(entries, own_key, low, top_value):
    longest = entries.shape.index(max(entries.shape))
    spots = []
    for shift in (0, 1):
        where = [jax.random.randint(jax.random.fold_in(own_key, axis), (), 0, length) for axis, length in enumerate(entries.shape)]
        where[longest] = (where[longest] + shift) % entries.shape[longest]
        spots.append(tuple(where))
    return entries.at[spots[0]].set(low).at[spots[1]].set(top_value)


def shard_levels(stream_key, extent, pieces, smallest, high):
    gain = 1.0
    for dim, parts in pieces:
        heights = jax.random.uniform(jax.random.fold_in(jax.random.fold_in(stream_key, 6), dim), (parts,), jnp.float32, smallest / len(pieces), high / len(pieces))
        gain = gain * jnp.repeat(jnp.exp(heights), extent[dim] // parts).reshape((-1,) + (1,) * (len(extent) - 1 - dim))
    return gain


def scatter_about(key, dims, width, bound, pieces=(), held_as=jnp.bfloat16):
    level = shard_levels(key, dims, pieces, -0.22, 0.18) if pieces else 1.0
    drawn = jax.random.normal(key, dims, jnp.float32) * width * level
    return jnp.minimum(jnp.maximum(drawn, -bound), bound).astype(held_as)


def setup_inputs(seed: int = 0) -> dict:
    keys = jax.random.split(jax.random.key(seed), 10)
    wind_east = scatter_about(keys[0], (L, NX, NY), 0.5, 3.0, ((0, 4), (1, 8)), jnp.float32)
    wind_north = scatter_about(keys[1], (L, NX, NY), 0.5, 3.0, ((0, 4), (1, 8)), jnp.float32)
    thickness = jnp.clip(jnp.exp(math.log(2.0) - 1.3862944 * jax.random.uniform(keys[2], (L, NX, NY), jnp.float32) ** shard_levels(keys[2], (L, NX, NY), ((0, 4), (1, 8)), -0.2, 0.2)), 0.5, 2.0)
    tracer_one = jnp.clip(1.0 * jax.random.uniform(keys[3], (L, NX, NY), jnp.float32) ** shard_levels(keys[3], (L, NX, NY), ((0, 4), (1, 8)), -0.2, 0.2), 0.0, 1.0)
    tracer_two = jnp.clip(jnp.exp(math.log(1.0) - 2.3025851 * jax.random.uniform(keys[4], (L, NX, NY), jnp.float32) ** shard_levels(keys[4], (L, NX, NY), ((0, 4), (1, 8)), -0.2, 0.2)), 0.1, 1.0)
    theta_step = jnp.clip(jnp.exp(jax.random.uniform(keys[5], (L,), jnp.float32, math.log(0.5), math.log(2.0))), 0.5, 2.0)
    surface_geopot = scatter_about(keys[6], (NX, NY), 2.0, 12.0, ((0, 8),), jnp.float32)
    map_factor = jnp.clip(jnp.exp(math.log(2.0) - 1.3862944 * jax.random.uniform(keys[7], (NX, NY), jnp.float32) ** shard_levels(keys[7], (NX, NY), ((0, 8),), -0.2, 0.2)), 0.5, 2.0)
    active_layers = plant(jax.random.randint(keys[8], (NX, NY), L // 2, L + 1), jax.random.fold_in(keys[8], 1), L // 2, L).astype(jnp.int32)
    return dict(wind_east=wind_east, wind_north=wind_north, thickness=thickness, tracer_one=tracer_one, tracer_two=tracer_two, theta_step=theta_step, surface_geopot=surface_geopot, map_factor=map_factor, active_layers=active_layers)


time_step = 0.05
top_pressure = 0.1
exner_power = 2.0 / 7.0


def potential_field(mass_field, theta_step, geopot):
    levels = mass_field.shape[0]
    pressure = top_pressure + jnp.cumsum(jnp.abs(mass_field), axis=0) / levels
    weighted = theta_step[:, None, None] * pressure ** exner_power
    summed = jnp.flip(jnp.cumsum(jnp.flip(weighted, 0), axis=0), 0)
    return geopot[None] + summed


def row_diff(values):
    return (jnp.roll(values, -1, 1) - jnp.roll(values, 1, 1)) * 0.5


def column_diff(values):
    padded = jnp.pad(values, ((0, 0), (0, 0), (1, 1)))
    return (padded[:, :, 2:] - padded[:, :, :-2]) * 0.5


def edge_diff(values):
    padded = jnp.pad(values, ((0, 0), (0, 0), (1, 1)), mode="edge")
    return (padded[:, :, 2:] - padded[:, :, :-2]) * 0.5


def tendency(fields, potential, metric, active, coriolis):
    east_mid, north_mid, mass_layer, tracer_first, tracer_last = fields[0], fields[1], fields[2], fields[3], fields[4]
    metric_mid = metric[None]
    flux_east = mass_layer * east_mid / metric_mid
    flux_north = mass_layer * north_mid / metric_mid
    d_mass = -(metric_mid * metric_mid) * (row_diff(flux_east) + column_diff(flux_north))

    def carried(values):
        return -metric_mid * (east_mid * row_diff(values) + north_mid * column_diff(values))

    d_east = carried(east_mid) + coriolis * north_mid - metric_mid * row_diff(potential)
    d_north = carried(north_mid) - coriolis * east_mid - metric_mid * edge_diff(potential)
    return jnp.stack([d_east, d_north, d_mass, carried(tracer_first), carried(tracer_last)]) * active[None]


def reference(wind_east, wind_north, thickness, tracer_one, tracer_two, theta_step, surface_geopot, map_factor, active_layers):
    levels = thickness.shape[0]
    columns = thickness.shape[2]
    layer_index = jnp.arange(levels, dtype=jnp.int32)[:, None, None]
    active = (layer_index < active_layers[None]).astype(jnp.float32)
    coriolis = 0.5 + jnp.arange(columns, dtype=jnp.float32)[None] / columns
    fields = jnp.stack([wind_east, wind_north, thickness, tracer_one, tracer_two])
    for outer_step in range(OUTER):
        potential = potential_field(fields[2], theta_step, surface_geopot)
        current = fields
        for fraction in (1.0 / 3.0, 0.5, 1.0):
            current = fields + (time_step * fraction) * tendency(current, potential, map_factor, active, coriolis)
        fields = current
    return fields[0], fields[1], fields[2], fields[3], fields[4]
```

```python
import functools

import jax
import jax.numpy as jnp
from jax import lax
from jax.experimental import pallas as pl
from jax.experimental.pallas import tpu as pltpu
from jax.sharding import PartitionSpec as P

OUTER = 2
FRACTIONS = (1.0 / 3.0, 0.5, 1.0)
LANES = 128

time_step = 0.05
top_pressure = 0.1
exner_power = 2.0 / 7.0

VMEM = pl.BlockSpec(memory_space=pltpu.VMEM)
SMEM = pl.BlockSpec(memory_space=pltpu.SMEM)
ANY = pl.BlockSpec(memory_space=pl.ANY)


class Geometry:
    def __init__(self, layers, rows, columns, levels):
        self.layers, self.rows, self.columns, self.levels = layers, rows, columns, levels
        self.sub = 2 * layers
        self.tiles = columns // LANES
        self.halo = OUTER * len(FRACTIONS)
        self.wide = rows + 2 * self.halo
        self.margin = 8
        self.plane = rows + 2 * self.margin
        assert self.sub == 8 and columns % LANES == 0 and rows % 8 == 0
        assert self.halo % 2 == 0 and self.halo <= self.margin <= rows


def lane(c):
    return pl.ds(c * LANES, LANES)


def sublane_index(g):
    return lax.broadcasted_iota(jnp.int32, (g.sub, LANES), 0)


def top_half(g):
    return sublane_index(g) < g.layers


def swap_halves(g, value):
    return pltpu.roll(value, g.layers, 0)


def column_differences(g, values, edge):
    lanes = lax.broadcasted_iota(jnp.int32, (g.sub, LANES), 1)
    first, last = lanes == 0, lanes == LANES - 1
    right_moved = [pltpu.roll(v, 1, 1) for v in values]
    left_moved = [pltpu.roll(v, LANES - 1, 1) for v in values]
    zero = jnp.zeros((g.sub, LANES), jnp.float32)
    result = []
    for c in range(g.tiles):
        before = right_moved[c - 1] if c > 0 else (values[c] if edge else zero)
        after = left_moved[c + 1] if c < g.tiles - 1 else (values[c] if edge else zero)
        result.append(
            jnp.where(last, after, left_moved[c]) - jnp.where(first, before, right_moved[c])
        )
    return result


def row_of(g, ref, e):
    return [ref[e, :, lane(c)] for c in range(g.tiles)]


def spread(flat, height, c, row):
    return flat[pl.ds(c * height + row, 8, stride=0), :]


def copy_fields(g, fields, scratch, sem):
    copies = []
    for slot, field in enumerate(fields):
        for c in range(g.tiles):
            copies.append(
                pltpu.make_async_copy(field.at[:, :, lane(c)], scratch.at[c, slot], sem)
            )
    return copies


def pack_kernel(g, u, v, h, q1, q2, metric, active, geopot,
                up, down, late_up, late_down, uv, hh, qq, mass, s_uv, s_hh, s_qq, sem):
    copies = (copy_fields(g, (h, h), s_hh, sem.at[0]) + copy_fields(g, (u, v), s_uv, sem.at[0])
              + copy_fields(g, (q1, q2), s_qq, sem.at[0]))
    for one in copies:
        one.start()
    for one in copies:
        one.wait()
    for c in range(g.tiles):
        total = jnp.abs(s_hh[c, 0, 0])
        for k in range(1, g.layers):
            total = total + jnp.abs(s_hh[c, 0, k])
        mass[:, lane(c)] = total
    block = g.sub * g.rows

    for source, target in ((s_uv, uv), (s_hh, hh), (s_qq, qq)):
        flat = source.reshape(g.tiles * block, LANES)

        def one_row(r, carry, flat=flat, target=target):
            for c in range(g.tiles):
                target[r, :, lane(c)] = flat[pl.ds(c * block + r, g.sub, stride=g.rows), :]
            return carry

        lax.fori_loop(0, g.rows, one_row, 0)
    top = top_half(g)
    n = g.halo
    for out, late, start, edge in ((up, late_up, g.rows - n, g.rows - g.margin),
                                   (down, late_down, 0, 0)):
        for c in range(g.tiles):
            for i in range(n):
                out[i, :, lane(c)] = uv[start + i, :, lane(c)]
                late[i, :, lane(c)] = qq[start + i, :, lane(c)]
            for i in range(n // 2):
                out[n + i, :, lane(c)] = jnp.where(
                    top, hh[start + 2 * i, :, lane(c)], hh[start + 2 * i + 1, :, lane(c)])
            span = pl.ds(edge, g.margin)
            out[n + n // 2, :, lane(c)] = metric[span, lane(c)]
            out[n + n // 2 + 1, :, lane(c)] = active[span, lane(c)].astype(jnp.float32)
            late[n, :, lane(c)] = geopot[span, lane(c)]


def exner_kernel(g, place, theta, h, gathered, weighted, below):
    me = place[0]
    count = gathered.shape[0]
    for c in range(g.tiles):
        running = jnp.zeros((g.rows, LANES), jnp.float32)
        for other in range(count):
            running = running + gathered[other, :, lane(c)] * jnp.where(other < me, 1.0, 0.0)
        terms = []
        for k in range(g.layers):
            running = running + jnp.abs(h[k, :, lane(c)])
            pressure = top_pressure + running * (1.0 / g.levels)
            terms.append(theta[me * g.layers + k] * jnp.exp(exner_power * jnp.log(pressure)))
        for k in range(g.layers - 2, -1, -1):
            terms[k] = terms[k] + terms[k + 1]
        for k in range(g.layers):
            weighted[k, :, lane(c)] = terms[k]
        below[:, lane(c)] = terms[0]


def montgomery_kernel(g, place, weighted, gathered, geopot, up, down, mm, s_mm):
    me = place[0]
    count = gathered.shape[0]
    block = g.sub * g.rows
    for c in range(g.tiles):
        offset = jnp.zeros((g.rows, LANES), jnp.float32)
        for other in range(count):
            offset = offset + gathered[other, :, lane(c)] * jnp.where(other > me, 1.0, 0.0)
        for k in range(g.layers):
            value = geopot[:, lane(c)] + (weighted[k, :, lane(c)] + offset)
            s_mm[c, 0, k] = value
            s_mm[c, 1, k] = value
    flat = s_mm.reshape(g.tiles * block, LANES)

    def one_row(r, carry):
        for c in range(g.tiles):
            mm[r, :, lane(c)] = flat[pl.ds(c * block + r, g.sub, stride=g.rows), :]
        return carry

    lax.fori_loop(0, g.rows, one_row, 0)
    top = top_half(g)
    for out, start in ((up, g.rows - g.halo), (down, 0)):
        for c in range(g.tiles):
            for i in range(g.halo // 2):
                out[i, :, lane(c)] = jnp.where(
                    top, mm[start + 2 * i, :, lane(c)], mm[start + 2 * i + 1, :, lane(c)])


def unpack_pair(g, top, value):
    other = swap_halves(g, value)
    return jnp.where(top, value, other), jnp.where(top, other, value)


def fill_planes(g, up, down, metric, active, s_metric, s_inverse, s_active):
    n = g.halo + g.halo // 2
    low, high = pl.ds(0, g.margin), pl.ds(g.margin + g.rows, g.margin)
    own = pl.ds(g.margin, g.rows)
    for c in range(g.tiles):
        for span, value, count in (
            (low, up[n, :, lane(c)], up[n + 1, :, lane(c)]),
            (own, metric[:, lane(c)], active[:, lane(c)].astype(jnp.float32)),
            (high, down[n, :, lane(c)], down[n + 1, :, lane(c)]),
        ):
            s_metric[c, span] = value
            s_inverse[c, span] = 1.0 / value
            s_active[c, span] = count


class Planes:
    def __init__(self, g, place, s_metric, s_inverse, s_active):
        self.g = g
        flat = lambda ref: ref.reshape(g.tiles * g.plane, LANES)
        self.metric_rows, self.inverse_rows = flat(s_metric), flat(s_inverse)
        self.active_rows = flat(s_active)
        self.shift = g.margin - g.halo
        layer = place[0] * g.layers + lax.rem(sublane_index(g), g.layers)
        self.layer = layer.astype(jnp.float32)

    def metric(self, e, c):
        return spread(self.metric_rows, self.g.plane, c, e + self.shift)

    def inverse(self, e, c):
        return spread(self.inverse_rows, self.g.plane, c, e + self.shift)

    def active(self, e, c, scale):
        count = spread(self.active_rows, self.g.plane, c, e + self.shift)
        return jnp.where(self.layer < count, scale, 0.0)


def signed_coriolis(g, c):
    column = (lax.broadcasted_iota(jnp.int32, (g.sub, LANES), 1) + c * LANES).astype(jnp.float32)
    f = 0.5 + column / g.columns
    return jnp.where(top_half(g), f, -f)


def section(g, planes, low, high, scale, uv, uv0, mass=None, tracer=None):
    top = top_half(g)

    def put(target, e, c, value):
        if target is None:
            return
        if callable(target):
            target(e, c, value)
        else:
            target[e, :, lane(c)] = value

    def one_row(e, carry):
        here = row_of(g, uv, e)
        if mass is not None:
            flux, hh0, gradient, coriolis, uv_out, flux_out, hh_out = mass
            uv_columns = column_differences(g, here, False)
            flux_columns = column_differences(g, row_of(g, flux, e), False)
        if tracer is not None:
            qq, qq0, qq_out = tracer
            qq_columns = column_differences(g, row_of(g, qq, e), False)
        for c in range(g.tiles):
            swapped = swap_halves(g, here[c])
            east = jnp.where(top, here[c], swapped)
            north = jnp.where(top, swapped, here[c])
            metric = planes.metric(e, c)
            live = planes.active(e, c, scale)
            carry_scale = live * (metric * -0.5)
            if tracer is not None:
                rows = qq[e + 1, :, lane(c)] - qq[e - 1, :, lane(c)]
                put(qq_out, e, c, qq0[e, :, lane(c)]
                    + carry_scale * (east * rows + north * qq_columns[c]))
            if mass is not None:
                rows = uv[e + 1, :, lane(c)] - uv[e - 1, :, lane(c)]
                uv_new = (uv0[e, :, lane(c)]
                          + carry_scale * (east * rows + north * uv_columns[c]
                                           + gradient[e, :, lane(c)])
                          + live * (coriolis[:, lane(c)] * swapped))
                put(uv_out, e, c, uv_new)
                rows = flux[e + 1, :, lane(c)] - flux[e - 1, :, lane(c)]
                mixed = jnp.where(top, rows, flux_columns[c])
                hh_new = hh0[e, :, lane(c)] + (carry_scale * metric) * (
                    mixed + swap_halves(g, mixed))
                put(hh_out, e, c, hh_new)
                if flux_out is not None:
                    put(flux_out, e, c, hh_new * uv_new * planes.inverse(e, c))
        return carry

    lax.fori_loop(low, high, one_row, 0)


def fill_flux(g, planes, low, high, uv, hh, flux):
    def one_row(e, carry):
        for c in range(g.tiles):
            flux[e, :, lane(c)] = (
                hh[e, :, lane(c)] * uv[e, :, lane(c)] * planes.inverse(e, c))
        return carry

    lax.fori_loop(low, high, one_row, 0)


def fill_gradient(g, low, high, mm, gradient):
    top = top_half(g)

    def one_row(e, carry):
        columns = column_differences(g, row_of(g, mm, e), True)
        for c in range(g.tiles):
            gradient[e, :, lane(c)] = jnp.where(
                top, mm[e + 1, :, lane(c)] - mm[e - 1, :, lane(c)], columns[c])
        return carry

    lax.fori_loop(low, high, one_row, 0)


def fill_coriolis(g, coriolis):
    for c in range(g.tiles):
        coriolis[:, lane(c)] = signed_coriolis(g, c)


def first_step_kernel(g, place, uv_own, hh_own, mm_own, up, down, m_up, m_down, metric, active,
                      uv0, uv1, uv2, uv3, hh3, mass,
                      hh0, mm, flux0, flux1, gradient, coriolis,
                      s_metric, s_inverse, s_active, sem):
    n = g.halo
    own = pl.ds(n, g.rows)
    copies = [
        pltpu.make_async_copy(uv_own, uv0.at[own], sem.at[0]),
        pltpu.make_async_copy(hh_own, hh0.at[own], sem.at[1]),
        pltpu.make_async_copy(mm_own, mm.at[own], sem.at[2]),
    ]
    for one in copies:
        one.start()
    fill_planes(g, up, down, metric, active, s_metric, s_inverse, s_active)
    fill_coriolis(g, coriolis)
    planes = Planes(g, place, s_metric, s_inverse, s_active)
    top = top_half(g)
    for halo, m_halo, start in ((up, m_up, 0), (down, m_down, n + g.rows)):
        for c in range(g.tiles):
            for i in range(n):
                uv0[start + i, :, lane(c)] = halo[i, :, lane(c)]
            for i in range(n // 2):
                for target, source in ((hh0, halo[n + i, :, lane(c)]),
                                       (mm, m_halo[i, :, lane(c)])):
                    one, two = unpack_pair(g, top, source)
                    target[start + 2 * i, :, lane(c)] = one
                    target[start + 2 * i + 1, :, lane(c)] = two
    for one in copies:
        one.wait()
    w = g.wide
    fill_flux(g, planes, 0, w, uv0, hh0, flux0)
    fill_gradient(g, 1, w - 1, mm, gradient)
    s = [time_step * fraction for fraction in FRACTIONS]
    section(g, planes, 1, w - 1, s[0], uv0, uv0,
            mass=(flux0, hh0, gradient, coriolis, uv1, flux1, None))
    section(g, planes, 2, w - 2, s[1], uv1, uv0,
            mass=(flux1, hh0, gradient, coriolis, uv2, flux0, None))
    first = len(FRACTIONS)

    section(g, planes, first, w - first, s[2], uv2, uv0,
            mass=(flux0, hh0, gradient, coriolis, uv3, None, hh3))
    fill_mass(g, first, w - first, hh3, mass)


def any_lane(c):
    return pl.ds(pl.multiple_of(c * LANES, LANES), LANES)


def fill_mass(g, low, high, hh, mass):
    place_in = sublane_index(g)

    def one_tile(c, carry):
        for start in range(0, mass.shape[0], g.sub):
            rows = jnp.zeros((g.sub, LANES), jnp.float32)
            for j in range(g.sub):
                e = low + start + j
                if e < high:
                    size = jnp.abs(hh[e, :, any_lane(c)])
                    size = size + pltpu.roll(size, 1, 0)
                    size = size + pltpu.roll(size, 2, 0)
                    rows = jnp.where(place_in == j, size, rows)
            mass[pl.ds(start, g.sub), any_lane(c)] = rows
        return carry

    lax.fori_loop(0, g.tiles, one_tile, 0)


def second_exner_kernel(g, place, theta, hh, gathered, weighted, below, s_offset):
    me = place[0]
    count = gathered.shape[0]
    height = s_offset.shape[1]
    for c in range(g.tiles):
        offset = jnp.zeros((height, LANES), jnp.float32)
        for other in range(count):
            offset = offset + gathered[other, :, lane(c)] * jnp.where(other < me, 1.0, 0.0)
        s_offset[c] = offset
    flat = s_offset.reshape(g.tiles * height, LANES)
    top = top_half(g)
    layer = lax.rem(sublane_index(g), g.layers)
    first = len(FRACTIONS)
    jump = jnp.zeros((g.sub, LANES), jnp.float32)
    for k in range(g.layers):
        jump = jnp.where(layer == k, theta[me * g.layers + k], jump)

    place_in = sublane_index(g)
    pairs = (g.wide - 2 * first) // 2

    def one_tile(c, carry):
        for start in range(0, height, g.sub):
            rows = jnp.zeros((g.sub, LANES), jnp.float32)
            for j in range(0, g.sub, 2):
                i = (start + j) // 2
                if i >= pairs:
                    continue
                e = first + 2 * i
                size = jnp.abs(jnp.where(top, hh[e, :, any_lane(c)], hh[e + 1, :, any_lane(c)]))
                size = size + jnp.where(layer >= 1, pltpu.roll(size, 1, 0), 0.0)
                size = size + jnp.where(layer >= 2, pltpu.roll(size, 2, 0), 0.0)
                offset = jnp.where(top, spread(flat, height, c, 2 * i),
                                   spread(flat, height, c, 2 * i + 1))
                pressure = top_pressure + (size + offset) * (1.0 / g.levels)
                term = jump * jnp.exp(exner_power * jnp.log(pressure))
                term = term + jnp.where(
                    layer < g.layers - 1, pltpu.roll(term, g.sub - 1, 0), 0.0)
                term = term + jnp.where(
                    layer < g.layers - 2, pltpu.roll(term, g.sub - 2, 0), 0.0)
                weighted[i, :, any_lane(c)] = term
                first_row = pltpu.roll(term, j, 0) if j else term
                rows = jnp.where(place_in == j, first_row, rows)
                rows = jnp.where(
                    place_in == j + 1, pltpu.roll(term, (j + 1 - g.layers) % g.sub, 0), rows)
            below[pl.ds(start, g.sub), any_lane(c)] = rows
        return carry

    lax.fori_loop(0, g.tiles, one_tile, 0)


def second_step_kernel(g, place, weighted, gathered, geopot, up, down, late_up, late_down,
                       metric, active, uv0, uv1, uv2, uv3, hh3, qq_own,
                       u_out, v_out, h_out, q1_out, q2_out,
                       qq0, qq1, qq2, qq3, mm, gradient, coriolis, flux0, flux1, uv4, uv5,
                       s_metric, s_inverse, s_active, s_geopot, s_offset,
                       s_uv, s_hh, s_qq, sem):
    n = g.halo
    first = len(FRACTIONS)
    w = g.wide
    s = [time_step * fraction for fraction in FRACTIONS]
    own_copy = pltpu.make_async_copy(qq_own, qq0.at[pl.ds(n, g.rows)], sem.at[0])
    own_copy.start()
    fill_planes(g, up, down, metric, active, s_metric, s_inverse, s_active)
    fill_coriolis(g, coriolis)
    planes = Planes(g, place, s_metric, s_inverse, s_active)
    top = top_half(g)
    for halo, start in ((late_up, 0), (late_down, n + g.rows)):
        for c in range(g.tiles):
            for i in range(n):
                qq0[start + i, :, lane(c)] = halo[i, :, lane(c)]
    me = place[0]
    count = gathered.shape[0]
    height = s_offset.shape[1]
    for c in range(g.tiles):
        s_geopot[c, pl.ds(0, g.margin)] = late_up[n, :, lane(c)]
        s_geopot[c, pl.ds(g.margin, g.rows)] = geopot[:, lane(c)]
        s_geopot[c, pl.ds(g.margin + g.rows, g.margin)] = late_down[n, :, lane(c)]
        offset = jnp.zeros((height, LANES), jnp.float32)
        for other in range(count):
            offset = offset + gathered[other, :, lane(c)] * jnp.where(other > me, 1.0, 0.0)
        s_offset[c] = offset
    geopot_rows = s_geopot.reshape(g.tiles * g.plane, LANES)
    offset_rows = s_offset.reshape(g.tiles * height, LANES)
    shift = g.margin - n

    def one_pair(i, carry):
        e = first + 2 * i
        for c in range(g.tiles):
            base = jnp.where(top, spread(geopot_rows, g.plane, c, e + shift),
                             spread(geopot_rows, g.plane, c, e + 1 + shift))
            offset = jnp.where(top, spread(offset_rows, height, c, 2 * i),
                               spread(offset_rows, height, c, 2 * i + 1))
            one, two = unpack_pair(g, top, base + (weighted[i, :, lane(c)] + offset))
            mm[e, :, lane(c)] = one
            mm[e + 1, :, lane(c)] = two
        return carry

    lax.fori_loop(0, (w - 2 * first) // 2, one_pair, 0)
    fill_gradient(g, first + 1, w - first - 1, mm, gradient)
    fill_flux(g, planes, first, w - first, uv3, hh3, flux0)
    own_copy.wait()
    section(g, planes, 1, w - 1, s[0], uv0, None, tracer=(qq0, qq0, qq1))
    section(g, planes, 2, w - 2, s[1], uv1, None, tracer=(qq1, qq0, qq2))
    section(g, planes, 3, w - 3, s[2], uv2, None, tracer=(qq2, qq0, qq3))
    section(g, planes, 4, w - 4, s[0], uv3, uv3, tracer=(qq3, qq3, qq1),
            mass=(flux0, hh3, gradient, coriolis, uv4, flux1, None))
    section(g, planes, 5, w - 5, s[1], uv4, uv3, tracer=(qq1, qq3, qq2),
            mass=(flux1, hh3, gradient, coriolis, uv5, flux0, None))
    block = g.sub * g.rows

    def store_in(scratch):
        flat = scratch.reshape(g.tiles * block, LANES)

        def store(e, c, value):
            flat[pl.ds(c * block + e - n, g.sub, stride=g.rows), :] = value

        return store

    section(g, planes, 6, w - 6, s[2], uv5, uv3, tracer=(qq2, qq3, store_in(s_qq)),
            mass=(flux0, hh3, gradient, coriolis, store_in(s_uv), None, store_in(s_hh)))
    copies = []
    for target, scratch, slot in ((u_out, s_uv, 0), (v_out, s_uv, 1), (h_out, s_hh, 0),
                                  (q1_out, s_qq, 0), (q2_out, s_qq, 1)):
        for c in range(g.tiles):
            copies.append(pltpu.make_async_copy(
                scratch.at[c, slot], target.at[:, :, lane(c)], sem.at[1]))
    for one in copies:
        one.start()
    for one in copies:
        one.wait()


def local(
    wind_east,
    wind_north,
    thickness,
    tracer_one,
    tracer_two,
    theta_step,
    surface_geopot,
    map_factor,
    active_layers,
):
    layers, rows, columns = thickness.shape
    g = Geometry(layers, rows, columns, layers * lax.axis_size("lev"))
    n, w = g.halo, g.wide
    first = len(FRACTIONS)
    height = -(-(w - 2 * first) // 8) * 8
    count = lax.axis_size("row")
    forward = [(i, (i + 1) % count) for i in range(count)]
    backward = [(i, (i - 1) % count) for i in range(count)]
    place = lax.axis_index("lev").astype(jnp.int32).reshape(1)

    def shape(*dims):
        return jax.ShapeDtypeStruct(dims, jnp.float32)

    def call(body, outs, ins, scratch, name, out_specs=None):
        return pl.pallas_call(
            functools.partial(body, g),
            out_shape=outs,
            in_specs=ins,
            out_specs=out_specs if out_specs is not None else [VMEM] * len(outs),
            scratch_shapes=scratch,
            name=name,
        )

    slab = shape(rows, g.sub, columns)
    broad = shape(w, g.sub, columns)
    fields = pltpu.VMEM((g.tiles, 2, layers, rows, LANES), jnp.float32)
    wide_scratch = pltpu.VMEM((w, g.sub, columns), jnp.float32)
    plane = pltpu.VMEM((g.tiles, g.plane, LANES), jnp.float32)
    offsets = pltpu.VMEM((g.tiles, height, LANES), jnp.float32)
    coriolis = pltpu.VMEM((g.sub, columns), jnp.float32)
    early = n + n // 2 + 2

    up, down, late_up, late_down, uv, hh, qq, mass = call(
        pack_kernel,
        [shape(early, g.sub, columns)] * 2 + [shape(n + 1, g.sub, columns)] * 2
        + [slab] * 3 + [shape(rows, columns)],
        [ANY] * 5 + [VMEM] * 3,
        [fields] * 3 + [pltpu.SemaphoreType.DMA((1,))],
        "pack",
    )(wind_east, wind_north, thickness, tracer_one, tracer_two,
      map_factor, active_layers, surface_geopot)
    up_in = lax.ppermute(up, "row", forward)
    down_in = lax.ppermute(down, "row", backward)
    weighted, below = call(
        exner_kernel, [shape(layers, rows, columns), shape(rows, columns)],
        [SMEM, SMEM, VMEM, VMEM], [], "exner",
    )(place, theta_step, thickness, lax.all_gather(mass, "lev"))
    m_up, m_down, mm = call(
        montgomery_kernel, [shape(n // 2, g.sub, columns)] * 2 + [slab],
        [SMEM, VMEM, VMEM, VMEM], [fields], "montgomery",
    )(place, weighted, lax.all_gather(below, "lev"), surface_geopot)
    m_up_in = lax.ppermute(m_up, "row", forward)
    m_down_in = lax.ppermute(m_down, "row", backward)
    uv0, uv1, uv2, uv3, hh3, mass = call(
        first_step_kernel, [broad] * 5 + [shape(height, columns)],
        [SMEM] + [ANY] * 3 + [VMEM] * 6,
        [wide_scratch] * 5 + [coriolis] + [plane] * 3 + [pltpu.SemaphoreType.DMA((3,))],
        "first_step",
    )(place, uv, hh, mm, up_in, down_in, m_up_in, m_down_in, map_factor, active_layers)
    late_up_in = lax.ppermute(late_up, "row", forward)
    late_down_in = lax.ppermute(late_down, "row", backward)
    weighted, below = call(
        second_exner_kernel,
        [shape((w - 2 * first) // 2, g.sub, columns), shape(height, columns)],
        [SMEM, SMEM, VMEM, VMEM], [offsets], "second_exner",
    )(place, theta_step, hh3, lax.all_gather(mass, "lev"))
    return tuple(call(
        second_step_kernel, [shape(layers, rows, columns)] * 5,
        [SMEM] + [VMEM] * 14 + [ANY],
        [wide_scratch] * 6 + [coriolis] + [wide_scratch] * 4 + [plane] * 4 + [offsets]
        + [fields] * 3 + [pltpu.SemaphoreType.DMA((2,))],
        "second_step", [ANY] * 5,
    )(place, weighted, lax.all_gather(below, "lev"), surface_geopot, up_in, down_in,
      late_up_in, late_down_in, map_factor, active_layers, uv0, uv1, uv2, uv3, hh3, qq))


def solution(mesh):
    state = P("lev", "row", None)
    flat = P("row", None)
    return jax.shard_map(
        local,
        mesh=mesh,
        in_specs=(state,) * 5 + (P(), flat, flat, flat),
        out_specs=(state,) * 5,
        check_vma=False,
    )
```

```python
import functools

import jax
import jax.numpy as jnp
from jax import lax
from jax.experimental import pallas as pl
from jax.experimental.pallas import tpu as pltpu
from jax.sharding import PartitionSpec as P

OUTER = 2
FRACTIONS = (1.0 / 3.0, 0.5, 1.0)
LANES = 128
SCOPED_BYTES = 24 * 1024 * 1024

time_step = 0.05
top_pressure = 0.1
exner_power = 2.0 / 7.0

VMEM = pl.BlockSpec(memory_space=pltpu.VMEM)
SMEM = pl.BlockSpec(memory_space=pltpu.SMEM)
ANY = pl.BlockSpec(memory_space=pl.ANY)


class Geometry:
    def __init__(self, layers, rows, columns, levels):
        self.layers, self.rows, self.columns, self.levels = layers, rows, columns, levels
        self.sub = 2 * layers
        self.tiles = columns // LANES
        self.halo = OUTER * len(FRACTIONS)
        self.wide = rows + 2 * self.halo
        self.margin = 8
        self.plane = rows + 2 * self.margin
        assert self.sub == 8 and columns % LANES == 0 and rows % 8 == 0
        assert self.halo % 2 == 0 and self.halo <= self.margin <= rows


def lane(c):
    return pl.ds(c * LANES, LANES)


def sublane_index(g):
    return lax.broadcasted_iota(jnp.int32, (g.sub, LANES), 0)


def top_half(g):
    return sublane_index(g) < g.layers


def swap_halves(g, value):
    return pltpu.roll(value, g.layers, 0)


def column_differences(g, values, edge):
    lanes = lax.broadcasted_iota(jnp.int32, (g.sub, LANES), 1)
    first, last = lanes == 0, lanes == LANES - 1
    right_moved = [pltpu.roll(v, 1, 1) for v in values]
    left_moved = [pltpu.roll(v, LANES - 1, 1) for v in values]
    zero = jnp.zeros((g.sub, LANES), jnp.float32)
    result = []
    for c in range(g.tiles):
        before = right_moved[c - 1] if c > 0 else (values[c] if edge else zero)
        after = left_moved[c + 1] if c < g.tiles - 1 else (values[c] if edge else zero)
        result.append(
            jnp.where(last, after, left_moved[c]) - jnp.where(first, before, right_moved[c])
        )
    return result


def row_of(g, ref, e):
    return [ref[e, :, lane(c)] for c in range(g.tiles)]


def spread(flat, height, c, row):
    return flat[pl.ds(c * height + row, 8, stride=0), :]


def copy_fields(g, fields, scratch, sem):
    copies = []
    for slot, field in enumerate(fields):
        for c in range(g.tiles):
            copies.append(
                pltpu.make_async_copy(field.at[:, :, lane(c)], scratch.at[c, slot], sem)
            )
    return copies


def pack_kernel(g, u, v, h, q1, q2, metric, active, geopot,
                up, down, late_up, late_down, uv, hh, qq, mass, s_uv, s_hh, s_qq, sem):
    copies = (copy_fields(g, (h, h), s_hh, sem.at[0]) + copy_fields(g, (u, v), s_uv, sem.at[0])
              + copy_fields(g, (q1, q2), s_qq, sem.at[0]))
    for one in copies:
        one.start()
    for one in copies:
        one.wait()
    for c in range(g.tiles):
        total = jnp.abs(s_hh[c, 0, 0])
        for k in range(1, g.layers):
            total = total + jnp.abs(s_hh[c, 0, k])
        mass[:, lane(c)] = total
    block = g.sub * g.rows

    for source, target in ((s_uv, uv), (s_hh, hh), (s_qq, qq)):
        flat = source.reshape(g.tiles * block, LANES)

        def one_row(r, carry, flat=flat, target=target):
            for c in range(g.tiles):
                target[r, :, lane(c)] = flat[pl.ds(c * block + r, g.sub, stride=g.rows), :]
            return carry

        lax.fori_loop(0, g.rows, one_row, 0)
    top = top_half(g)
    n = g.halo
    for out, late, start, edge in ((up, late_up, g.rows - n, g.rows - g.margin),
                                   (down, late_down, 0, 0)):
        for c in range(g.tiles):
            for i in range(n):
                out[i, :, lane(c)] = uv[start + i, :, lane(c)]
                late[i, :, lane(c)] = qq[start + i, :, lane(c)]
            for i in range(n // 2):
                out[n + i, :, lane(c)] = jnp.where(
                    top, hh[start + 2 * i, :, lane(c)], hh[start + 2 * i + 1, :, lane(c)])
            span = pl.ds(edge, g.margin)
            out[n + n // 2, :, lane(c)] = metric[span, lane(c)]
            out[n + n // 2 + 1, :, lane(c)] = active[span, lane(c)].astype(jnp.float32)
            late[n, :, lane(c)] = geopot[span, lane(c)]


def exner_kernel(g, place, theta, h, gathered, weighted, below):
    me = place[0]
    count = gathered.shape[0]
    for c in range(g.tiles):
        running = jnp.zeros((g.rows, LANES), jnp.float32)
        for other in range(count):
            running = running + gathered[other, :, lane(c)] * jnp.where(other < me, 1.0, 0.0)
        terms = []
        for k in range(g.layers):
            running = running + jnp.abs(h[k, :, lane(c)])
            pressure = top_pressure + running * (1.0 / g.levels)
            terms.append(theta[me * g.layers + k] * jnp.exp(exner_power * jnp.log(pressure)))
        for k in range(g.layers - 2, -1, -1):
            terms[k] = terms[k] + terms[k + 1]
        for k in range(g.layers):
            weighted[k, :, lane(c)] = terms[k]
        below[:, lane(c)] = terms[0]


def montgomery_kernel(g, place, weighted, gathered, geopot, up, down, mm, s_mm):
    me = place[0]
    count = gathered.shape[0]
    block = g.sub * g.rows
    for c in range(g.tiles):
        offset = jnp.zeros((g.rows, LANES), jnp.float32)
        for other in range(count):
            offset = offset + gathered[other, :, lane(c)] * jnp.where(other > me, 1.0, 0.0)
        for k in range(g.layers):
            value = geopot[:, lane(c)] + (weighted[k, :, lane(c)] + offset)
            s_mm[c, 0, k] = value
            s_mm[c, 1, k] = value
    flat = s_mm.reshape(g.tiles * block, LANES)

    def one_row(r, carry):
        for c in range(g.tiles):
            mm[r, :, lane(c)] = flat[pl.ds(c * block + r, g.sub, stride=g.rows), :]
        return carry

    lax.fori_loop(0, g.rows, one_row, 0)
    top = top_half(g)
    for out, start in ((up, g.rows - g.halo), (down, 0)):
        for c in range(g.tiles):
            for i in range(g.halo // 2):
                out[i, :, lane(c)] = jnp.where(
                    top, mm[start + 2 * i, :, lane(c)], mm[start + 2 * i + 1, :, lane(c)])


def unpack_pair(g, top, value):
    other = swap_halves(g, value)
    return jnp.where(top, value, other), jnp.where(top, other, value)


def fill_planes(g, up, down, metric, active, s_metric, s_inverse, s_active):
    n = g.halo + g.halo // 2
    low, high = pl.ds(0, g.margin), pl.ds(g.margin + g.rows, g.margin)
    own = pl.ds(g.margin, g.rows)
    for c in range(g.tiles):
        for span, value, count in (
            (low, up[n, :, lane(c)], up[n + 1, :, lane(c)]),
            (own, metric[:, lane(c)], active[:, lane(c)].astype(jnp.float32)),
            (high, down[n, :, lane(c)], down[n + 1, :, lane(c)]),
        ):
            s_metric[c, span] = value
            s_inverse[c, span] = 1.0 / value
            s_active[c, span] = count


class Planes:
    def __init__(self, g, place, s_metric, s_inverse, s_active):
        self.g = g
        flat = lambda ref: ref.reshape(g.tiles * g.plane, LANES)
        self.metric_rows, self.inverse_rows = flat(s_metric), flat(s_inverse)
        self.active_rows = flat(s_active)
        self.shift = g.margin - g.halo
        layer = place[0] * g.layers + lax.rem(sublane_index(g), g.layers)
        self.layer = layer.astype(jnp.float32)

    def metric(self, e, c):
        return spread(self.metric_rows, self.g.plane, c, e + self.shift)

    def inverse(self, e, c):
        return spread(self.inverse_rows, self.g.plane, c, e + self.shift)

    def active(self, e, c, scale):
        count = spread(self.active_rows, self.g.plane, c, e + self.shift)
        return jnp.where(self.layer < count, scale, 0.0)


def signed_coriolis(g, c):
    column = (lax.broadcasted_iota(jnp.int32, (g.sub, LANES), 1) + c * LANES).astype(jnp.float32)
    f = 0.5 + column / g.columns
    return jnp.where(top_half(g), f, -f)


def section(g, planes, low, high, scale, uv, uv0, mass=None, tracer=None):
    top = top_half(g)

    def put(target, e, c, value):
        if target is None:
            return
        if callable(target):
            target(e, c, value)
        else:
            target[e, :, lane(c)] = value

    def one_row(e, carry):
        here = row_of(g, uv, e)
        if mass is not None:
            flux, hh0, gradient, coriolis, uv_out, flux_out, hh_out = mass
            uv_columns = column_differences(g, here, False)
            flux_columns = column_differences(g, row_of(g, flux, e), False)
        if tracer is not None:
            qq, qq0, qq_out = tracer
            qq_columns = column_differences(g, row_of(g, qq, e), False)
        for c in range(g.tiles):
            swapped = swap_halves(g, here[c])
            east = jnp.where(top, here[c], swapped)
            north = jnp.where(top, swapped, here[c])
            metric = planes.metric(e, c)
            live = planes.active(e, c, scale)
            carry_scale = live * (metric * -0.5)
            if tracer is not None:
                rows = qq[e + 1, :, lane(c)] - qq[e - 1, :, lane(c)]
                put(qq_out, e, c, qq0[e, :, lane(c)]
                    + carry_scale * (east * rows + north * qq_columns[c]))
            if mass is not None:
                rows = uv[e + 1, :, lane(c)] - uv[e - 1, :, lane(c)]
                uv_new = (uv0[e, :, lane(c)]
                          + carry_scale * (east * rows + north * uv_columns[c]
                                           + gradient[e, :, lane(c)])
                          + live * (coriolis[:, lane(c)] * swapped))
                put(uv_out, e, c, uv_new)
                rows = flux[e + 1, :, lane(c)] - flux[e - 1, :, lane(c)]
                mixed = jnp.where(top, rows, flux_columns[c])
                hh_new = hh0[e, :, lane(c)] + (carry_scale * metric) * (
                    mixed + swap_halves(g, mixed))
                put(hh_out, e, c, hh_new)
                if flux_out is not None:
                    put(flux_out, e, c, hh_new * uv_new * planes.inverse(e, c))
        return carry

    lax.fori_loop(low, high, one_row, 0)


def fill_flux(g, planes, low, high, uv, hh, flux):
    def one_row(e, carry):
        for c in range(g.tiles):
            flux[e, :, lane(c)] = (
                hh[e, :, lane(c)] * uv[e, :, lane(c)] * planes.inverse(e, c))
        return carry

    lax.fori_loop(low, high, one_row, 0)


def fill_gradient(g, low, high, mm, gradient):
    top = top_half(g)

    def one_row(e, carry):
        columns = column_differences(g, row_of(g, mm, e), True)
        for c in range(g.tiles):
            gradient[e, :, lane(c)] = jnp.where(
                top, mm[e + 1, :, lane(c)] - mm[e - 1, :, lane(c)], columns[c])
        return carry

    lax.fori_loop(low, high, one_row, 0)


def fill_coriolis(g, coriolis):
    for c in range(g.tiles):
        coriolis[:, lane(c)] = signed_coriolis(g, c)


def first_step_kernel(g, place, uv_own, hh_own, mm_own, up, down, m_up, m_down, metric, active,
                      uv0, uv1, uv2, uv3, hh3, mass,
                      hh0, mm, flux0, flux1, gradient, coriolis,
                      s_metric, s_inverse, s_active, sem):
    n = g.halo
    own = pl.ds(n, g.rows)
    copies = [
        pltpu.make_async_copy(uv_own, uv0.at[own], sem.at[0]),
        pltpu.make_async_copy(hh_own, hh0.at[own], sem.at[1]),
        pltpu.make_async_copy(mm_own, mm.at[own], sem.at[2]),
    ]
    for one in copies:
        one.start()
    fill_planes(g, up, down, metric, active, s_metric, s_inverse, s_active)
    fill_coriolis(g, coriolis)
    planes = Planes(g, place, s_metric, s_inverse, s_active)
    top = top_half(g)
    for halo, m_halo, start in ((up, m_up, 0), (down, m_down, n + g.rows)):
        for c in range(g.tiles):
            for i in range(n):
                uv0[start + i, :, lane(c)] = halo[i, :, lane(c)]
            for i in range(n // 2):
                for target, source in ((hh0, halo[n + i, :, lane(c)]),
                                       (mm, m_halo[i, :, lane(c)])):
                    one, two = unpack_pair(g, top, source)
                    target[start + 2 * i, :, lane(c)] = one
                    target[start + 2 * i + 1, :, lane(c)] = two
    for one in copies:
        one.wait()
    w = g.wide
    fill_flux(g, planes, 0, w, uv0, hh0, flux0)
    fill_gradient(g, 1, w - 1, mm, gradient)
    s = [time_step * fraction for fraction in FRACTIONS]
    section(g, planes, 1, w - 1, s[0], uv0, uv0,
            mass=(flux0, hh0, gradient, coriolis, uv1, flux1, None))
    section(g, planes, 2, w - 2, s[1], uv1, uv0,
            mass=(flux1, hh0, gradient, coriolis, uv2, flux0, None))
    first = len(FRACTIONS)

    section(g, planes, first, w - first, s[2], uv2, uv0,
            mass=(flux0, hh0, gradient, coriolis, uv3, None, hh3))
    fill_mass(g, first, w - first, hh3, mass)


def any_lane(c):
    return pl.ds(pl.multiple_of(c * LANES, LANES), LANES)


def fill_mass(g, low, high, hh, mass):
    place_in = sublane_index(g)

    def one_tile(c, carry):
        for start in range(0, mass.shape[0], g.sub):
            rows = jnp.zeros((g.sub, LANES), jnp.float32)
            for j in range(g.sub):
                e = low + start + j
                if e < high:
                    size = jnp.abs(hh[e, :, any_lane(c)])
                    size = size + pltpu.roll(size, 1, 0)
                    size = size + pltpu.roll(size, 2, 0)
                    rows = jnp.where(place_in == j, size, rows)
            mass[pl.ds(start, g.sub), any_lane(c)] = rows
        return carry

    lax.fori_loop(0, g.tiles, one_tile, 0)


def second_exner_kernel(g, place, theta, hh, gathered, weighted, below, s_offset):
    me = place[0]
    count = gathered.shape[0]
    height = s_offset.shape[1]
    for c in range(g.tiles):
        offset = jnp.zeros((height, LANES), jnp.float32)
        for other in range(count):
            offset = offset + gathered[other, :, lane(c)] * jnp.where(other < me, 1.0, 0.0)
        s_offset[c] = offset
    flat = s_offset.reshape(g.tiles * height, LANES)
    top = top_half(g)
    layer = lax.rem(sublane_index(g), g.layers)
    first = len(FRACTIONS)
    jump = jnp.zeros((g.sub, LANES), jnp.float32)
    for k in range(g.layers):
        jump = jnp.where(layer == k, theta[me * g.layers + k], jump)

    place_in = sublane_index(g)
    pairs = (g.wide - 2 * first) // 2

    def one_tile(c, carry):
        for start in range(0, height, g.sub):
            rows = jnp.zeros((g.sub, LANES), jnp.float32)
            for j in range(0, g.sub, 2):
                i = (start + j) // 2
                if i >= pairs:
                    continue
                e = first + 2 * i
                size = jnp.abs(jnp.where(top, hh[e, :, any_lane(c)], hh[e + 1, :, any_lane(c)]))
                size = size + jnp.where(layer >= 1, pltpu.roll(size, 1, 0), 0.0)
                size = size + jnp.where(layer >= 2, pltpu.roll(size, 2, 0), 0.0)
                offset = jnp.where(top, spread(flat, height, c, 2 * i),
                                   spread(flat, height, c, 2 * i + 1))
                pressure = top_pressure + (size + offset) * (1.0 / g.levels)
                term = jump * jnp.exp(exner_power * jnp.log(pressure))
                term = term + jnp.where(
                    layer < g.layers - 1, pltpu.roll(term, g.sub - 1, 0), 0.0)
                term = term + jnp.where(
                    layer < g.layers - 2, pltpu.roll(term, g.sub - 2, 0), 0.0)
                weighted[i, :, any_lane(c)] = term
                first_row = pltpu.roll(term, j, 0) if j else term
                rows = jnp.where(place_in == j, first_row, rows)
                rows = jnp.where(
                    place_in == j + 1, pltpu.roll(term, (j + 1 - g.layers) % g.sub, 0), rows)
            below[pl.ds(start, g.sub), any_lane(c)] = rows
        return carry

    lax.fori_loop(0, g.tiles, one_tile, 0)


def second_step_kernel(g, place, weighted, gathered, geopot, up, down, late_up, late_down,
                       metric, active, uv0, uv1, uv2, uv3, hh3, qq_own,
                       u_out, v_out, h_out, q1_out, q2_out,
                       qq0, qq1, qq2, qq3, mm, gradient, coriolis, flux0, flux1, uv4, uv5,
                       s_metric, s_inverse, s_active, s_geopot, s_offset,
                       s_uv, s_hh, s_qq, sem):
    n = g.halo
    first = len(FRACTIONS)
    w = g.wide
    s = [time_step * fraction for fraction in FRACTIONS]
    own_copy = pltpu.make_async_copy(qq_own, qq0.at[pl.ds(n, g.rows)], sem.at[0])
    own_copy.start()
    fill_planes(g, up, down, metric, active, s_metric, s_inverse, s_active)
    fill_coriolis(g, coriolis)
    planes = Planes(g, place, s_metric, s_inverse, s_active)
    top = top_half(g)
    for halo, start in ((late_up, 0), (late_down, n + g.rows)):
        for c in range(g.tiles):
            for i in range(n):
                qq0[start + i, :, lane(c)] = halo[i, :, lane(c)]
    me = place[0]
    count = gathered.shape[0]
    height = s_offset.shape[1]
    for c in range(g.tiles):
        s_geopot[c, pl.ds(0, g.margin)] = late_up[n, :, lane(c)]
        s_geopot[c, pl.ds(g.margin, g.rows)] = geopot[:, lane(c)]
        s_geopot[c, pl.ds(g.margin + g.rows, g.margin)] = late_down[n, :, lane(c)]
        offset = jnp.zeros((height, LANES), jnp.float32)
        for other in range(count):
            offset = offset + gathered[other, :, lane(c)] * jnp.where(other > me, 1.0, 0.0)
        s_offset[c] = offset
    geopot_rows = s_geopot.reshape(g.tiles * g.plane, LANES)
    offset_rows = s_offset.reshape(g.tiles * height, LANES)
    shift = g.margin - n

    def one_pair(i, carry):
        e = first + 2 * i
        for c in range(g.tiles):
            base = jnp.where(top, spread(geopot_rows, g.plane, c, e + shift),
                             spread(geopot_rows, g.plane, c, e + 1 + shift))
            offset = jnp.where(top, spread(offset_rows, height, c, 2 * i),
                               spread(offset_rows, height, c, 2 * i + 1))
            one, two = unpack_pair(g, top, base + (weighted[i, :, lane(c)] + offset))
            mm[e, :, lane(c)] = one
            mm[e + 1, :, lane(c)] = two
        return carry

    lax.fori_loop(0, (w - 2 * first) // 2, one_pair, 0)
    fill_gradient(g, first + 1, w - first - 1, mm, gradient)
    fill_flux(g, planes, first, w - first, uv3, hh3, flux0)
    own_copy.wait()
    section(g, planes, 1, w - 1, s[0], uv0, None, tracer=(qq0, qq0, qq1))
    section(g, planes, 2, w - 2, s[1], uv1, None, tracer=(qq1, qq0, qq2))
    section(g, planes, 3, w - 3, s[2], uv2, None, tracer=(qq2, qq0, qq3))
    section(g, planes, 4, w - 4, s[0], uv3, uv3, tracer=(qq3, qq3, qq1),
            mass=(flux0, hh3, gradient, coriolis, uv4, flux1, None))
    section(g, planes, 5, w - 5, s[1], uv4, uv3, tracer=(qq1, qq3, qq2),
            mass=(flux1, hh3, gradient, coriolis, uv5, flux0, None))
    block = g.sub * g.rows

    def store_in(scratch):
        flat = scratch.reshape(g.tiles * block, LANES)

        def store(e, c, value):
            flat[pl.ds(c * block + e - n, g.sub, stride=g.rows), :] = value

        return store

    section(g, planes, 6, w - 6, s[2], uv5, uv3, tracer=(qq2, qq3, store_in(s_qq)),
            mass=(flux0, hh3, gradient, coriolis, store_in(s_uv), None, store_in(s_hh)))
    copies = []
    for target, scratch, slot in ((u_out, s_uv, 0), (v_out, s_uv, 1), (h_out, s_hh, 0),
                                  (q1_out, s_qq, 0), (q2_out, s_qq, 1)):
        for c in range(g.tiles):
            copies.append(pltpu.make_async_copy(
                scratch.at[c, slot], target.at[:, :, lane(c)], sem.at[1]))
    for one in copies:
        one.start()
    for one in copies:
        one.wait()


def local(
    wind_east,
    wind_north,
    thickness,
    tracer_one,
    tracer_two,
    theta_step,
    surface_geopot,
    map_factor,
    active_layers,
):
    layers, rows, columns = thickness.shape
    g = Geometry(layers, rows, columns, layers * lax.axis_size("lev"))
    n, w = g.halo, g.wide
    first = len(FRACTIONS)
    height = -(-(w - 2 * first) // 8) * 8
    count = lax.axis_size("row")
    forward = [(i, (i + 1) % count) for i in range(count)]
    backward = [(i, (i - 1) % count) for i in range(count)]
    place = lax.axis_index("lev").astype(jnp.int32).reshape(1)

    def shape(*dims):
        return pltpu.VMEM(dims, jnp.float32)

    def near(value):
        return pltpu.with_memory_space_constraint(value, pltpu.VMEM)

    def call(body, outs, ins, scratch, name, out_specs=None):
        return pl.pallas_call(
            functools.partial(body, g),
            out_shape=outs,
            in_specs=ins,
            out_specs=out_specs if out_specs is not None else [VMEM] * len(outs),
            scratch_shapes=scratch,
            compiler_params=pltpu.CompilerParams(vmem_limit_bytes=SCOPED_BYTES),
            name=name,
        )

    slab = shape(rows, g.sub, columns)
    broad = shape(w, g.sub, columns)
    fields = pltpu.VMEM((g.tiles, 2, layers, rows, LANES), jnp.float32)
    wide_scratch = pltpu.VMEM((w, g.sub, columns), jnp.float32)
    plane = pltpu.VMEM((g.tiles, g.plane, LANES), jnp.float32)
    offsets = pltpu.VMEM((g.tiles, height, LANES), jnp.float32)
    coriolis = pltpu.VMEM((g.sub, columns), jnp.float32)
    early = n + n // 2 + 2

    up, down, late_up, late_down, uv, hh, qq, mass = call(
        pack_kernel,
        [shape(early, g.sub, columns)] * 2 + [shape(n + 1, g.sub, columns)] * 2
        + [slab] * 3 + [shape(rows, columns)],
        [ANY] * 5 + [VMEM] * 3,
        [fields] * 3 + [pltpu.SemaphoreType.DMA((1,))],
        "pack",
    )(wind_east, wind_north, thickness, tracer_one, tracer_two,
      map_factor, active_layers, surface_geopot)
    up_in = near(lax.ppermute(up, "row", forward))
    down_in = near(lax.ppermute(down, "row", backward))
    weighted, below = call(
        exner_kernel, [shape(layers, rows, columns), shape(rows, columns)],
        [SMEM, SMEM, VMEM, VMEM], [], "exner",
    )(place, theta_step, thickness, near(lax.all_gather(mass, "lev")))
    m_up, m_down, mm = call(
        montgomery_kernel, [shape(n // 2, g.sub, columns)] * 2 + [slab],
        [SMEM, VMEM, VMEM, VMEM], [fields], "montgomery",
    )(place, weighted, near(lax.all_gather(below, "lev")), surface_geopot)
    m_up_in = near(lax.ppermute(m_up, "row", forward))
    m_down_in = near(lax.ppermute(m_down, "row", backward))
    uv0, uv1, uv2, uv3, hh3, mass = call(
        first_step_kernel, [broad] * 5 + [shape(height, columns)],
        [SMEM] + [ANY] * 3 + [VMEM] * 6,
        [wide_scratch] * 5 + [coriolis] + [plane] * 3 + [pltpu.SemaphoreType.DMA((3,))],
        "first_step",
    )(place, uv, hh, mm, up_in, down_in, m_up_in, m_down_in, map_factor, active_layers)
    late_up_in = near(lax.ppermute(late_up, "row", forward))
    late_down_in = near(lax.ppermute(late_down, "row", backward))
    weighted, below = call(
        second_exner_kernel,
        [shape((w - 2 * first) // 2, g.sub, columns), shape(height, columns)],
        [SMEM, SMEM, VMEM, VMEM], [offsets], "second_exner",
    )(place, theta_step, hh3, near(lax.all_gather(mass, "lev")))
    return tuple(call(
        second_step_kernel, [jax.ShapeDtypeStruct((layers, rows, columns), jnp.float32)] * 5,
        [SMEM] + [VMEM] * 14 + [ANY],
        [wide_scratch] * 6 + [coriolis] + [wide_scratch] * 4 + [plane] * 4 + [offsets]
        + [fields] * 3 + [pltpu.SemaphoreType.DMA((2,))],
        "second_step", [ANY] * 5,
    )(place, weighted, near(lax.all_gather(below, "lev")), surface_geopot, up_in, down_in,
      late_up_in, late_down_in, map_factor, active_layers, uv0, uv1, uv2, uv3, hh3, qq))


def solution(mesh):
    state = P("lev", "row", None)
    flat = P("row", None)
    return jax.shard_map(
        local,
        mesh=mesh,
        in_specs=(state,) * 5 + (P(), flat, flat, flat),
        out_specs=(state,) * 5,
        check_vma=False,
    )
```

```python
import functools

import jax
import jax.numpy as jnp
from jax import lax
from jax.experimental import pallas as pl
from jax.experimental.pallas import tpu as pltpu
from jax.sharding import PartitionSpec as P

OUTER = 2
FRACTIONS = (1.0 / 3.0, 0.5, 1.0)
LANES = 128
SCOPED_BYTES = 16 * 1024 * 1024

time_step = 0.05
top_pressure = 0.1
exner_power = 2.0 / 7.0

VMEM = pl.BlockSpec(memory_space=pltpu.VMEM)
SMEM = pl.BlockSpec(memory_space=pltpu.SMEM)
FAR = pl.BlockSpec(memory_space=pltpu.HBM)


class Geometry:
    def __init__(self, layers, rows, columns, levels):
        self.layers, self.rows, self.columns, self.levels = layers, rows, columns, levels
        self.sub = 2 * layers
        self.tiles = columns // LANES
        self.halo = OUTER * len(FRACTIONS)
        self.wide = rows + 2 * self.halo
        self.margin = 8
        self.plane = rows + 2 * self.margin
        assert self.sub == 8 and columns % LANES == 0 and rows % 8 == 0
        assert self.halo % 2 == 0 and self.halo <= self.margin <= rows


def lane(c):
    return pl.ds(c * LANES, LANES)


def sublane_index(g):
    return lax.broadcasted_iota(jnp.int32, (g.sub, LANES), 0)


def top_half(g):
    return sublane_index(g) < g.layers


def swap_halves(g, value):
    return pltpu.roll(value, g.layers, 0)


def column_differences(g, values, edge):
    lanes = lax.broadcasted_iota(jnp.int32, (g.sub, LANES), 1)
    first, last = lanes == 0, lanes == LANES - 1
    right_moved = [pltpu.roll(v, 1, 1) for v in values]
    left_moved = [pltpu.roll(v, LANES - 1, 1) for v in values]
    zero = jnp.zeros((g.sub, LANES), jnp.float32)
    result = []
    for c in range(g.tiles):
        before = right_moved[c - 1] if c > 0 else (values[c] if edge else zero)
        after = left_moved[c + 1] if c < g.tiles - 1 else (values[c] if edge else zero)
        result.append(
            jnp.where(last, after, left_moved[c]) - jnp.where(first, before, right_moved[c])
        )
    return result


def row_of(g, ref, e):
    return [ref[e, :, lane(c)] for c in range(g.tiles)]


def spread(flat, height, c, row):
    return flat[pl.ds(c * height + row, 8, stride=0), :]


def copy_fields(g, fields, scratch, sem):
    copies = []
    for slot, field in enumerate(fields):
        for c in range(g.tiles):
            copies.append(
                pltpu.make_async_copy(field.at[:, :, lane(c)], scratch.at[c, slot], sem)
            )
    return copies


def pack_kernel(g, u, v, h, q1, q2, metric, active, geopot, theta,
                up, down, late_up, late_down, uv, hh, qq, mass, own_metric, own_active, jumps,
                s_uv, s_hh, s_qq, s_active, s_geopot, s_theta, sem):
    copies = (copy_fields(g, (h, h), s_hh, sem.at[0]) + copy_fields(g, (u, v), s_uv, sem.at[0])
              + [pltpu.make_async_copy(metric, own_metric, sem.at[0]),
                 pltpu.make_async_copy(active, s_active, sem.at[0])])
    others = copy_fields(g, (q1, q2), s_qq, sem.at[1]) + [
        pltpu.make_async_copy(geopot, s_geopot, sem.at[1]),
        pltpu.make_async_copy(theta, s_theta, sem.at[2])]
    for one in copies + others:
        one.start()
    for one in copies:
        one.wait()
    for c in range(g.tiles):
        total = jnp.abs(s_hh[c, 0, 0])
        for k in range(1, g.layers):
            total = total + jnp.abs(s_hh[c, 0, k])
        mass[:, lane(c)] = total
        own_active[:, lane(c)] = s_active[:, lane(c)].astype(jnp.float32)
    block = g.sub * g.rows

    def gather_rows(source, target):
        flat = source.reshape(g.tiles * block, LANES)

        def one_row(r, carry):
            for c in range(g.tiles):
                target[r, :, lane(c)] = flat[pl.ds(c * block + r, g.sub, stride=g.rows), :]
            return carry

        lax.fori_loop(0, g.rows, one_row, 0, unroll=2)

    gather_rows(s_uv, uv)
    gather_rows(s_hh, hh)
    top = top_half(g)
    n = g.halo
    sides = ((up, late_up, g.rows - n, g.rows - g.margin), (down, late_down, 0, 0))
    for out, late, start, edge in sides:
        for c in range(g.tiles):
            for i in range(n):
                out[i, :, lane(c)] = uv[start + i, :, lane(c)]
            for i in range(n // 2):
                out[n + i, :, lane(c)] = jnp.where(
                    top, hh[start + 2 * i, :, lane(c)], hh[start + 2 * i + 1, :, lane(c)])
            span = pl.ds(edge, g.margin)
            out[n + n // 2, :, lane(c)] = own_metric[span, lane(c)]
            out[n + n // 2 + 1, :, lane(c)] = own_active[span, lane(c)]
    for one in others:
        one.wait()
    gather_rows(s_qq, qq)
    for out, late, start, edge in sides:
        for c in range(g.tiles):
            for i in range(n):
                late[i, :, lane(c)] = qq[start + i, :, lane(c)]
            late[n, :, lane(c)] = s_geopot[pl.ds(edge, g.margin), lane(c)]
    for k in range(g.levels):
        jumps[k] = jnp.full((g.sub, LANES), s_theta[k], jnp.float32)


def chip_mass_kernel(g, mass, other, total):
    for c in range(g.tiles):
        value = mass[:, lane(c)]
        for k in range(g.layers):
            value = value + jnp.abs(other[k, :, lane(c)])
        total[:, lane(c)] = value


def switches(me):
    high = me // 2
    odd = me - 2 * high
    return [jnp.where(flag, 1.0, 0.0) for flag in (high == 1, high == 0, odd == 1, odd == 0)]


def exner_kernel(g, place, jumps, own, other, above, weighted, chip_sum):
    me = place[0]
    partner = me + 1 - 2 * lax.rem(me, 2)
    low_chip, high_chip, low_group, high_group = switches(me)
    kinds = g.rows // g.sub

    def group(field, owner, offset, c, r):
        running = offset
        terms = []
        for k in range(g.layers):
            running = running + jnp.abs(field[k, pl.ds(r * g.sub, g.sub), lane(c)])
            pressure = top_pressure + running * (1.0 / g.levels)
            terms.append(jumps[owner * g.layers + k] * jnp.exp(exner_power * jnp.log(pressure)))
        for k in range(g.layers - 2, -1, -1):
            terms[k] = terms[k] + terms[k + 1]
        return terms

    def size(field, c, r):
        total = jnp.abs(field[0, pl.ds(r * g.sub, g.sub), lane(c)])
        for k in range(1, g.layers):
            total = total + jnp.abs(field[k, pl.ds(r * g.sub, g.sub), lane(c)])
        return total

    for c in range(g.tiles):
        for r in range(kinds):
            rows = pl.ds(r * g.sub, g.sub)
            outer = above[rows, lane(c)] * low_chip
            mine = group(own, me, outer + size(other, c, r) * low_group, c, r)
            theirs = group(other, partner, outer + size(own, c, r) * high_group, c, r)
            for k in range(g.layers):
                weighted[k, rows, lane(c)] = mine[k] + theirs[0] * high_group
            chip_sum[rows, lane(c)] = mine[0] + theirs[0]


def montgomery_kernel(g, place, weighted, beneath, geopot, up, down, mm, s_mm):
    high_chip = switches(place[0])[1]
    block = g.sub * g.rows
    for c in range(g.tiles):
        base = beneath[:, lane(c)] * high_chip
        for k in range(g.layers):
            value = geopot[:, lane(c)] + (weighted[k, :, lane(c)] + base)
            s_mm[c, 0, k] = value
            s_mm[c, 1, k] = value
    flat = s_mm.reshape(g.tiles * block, LANES)

    def one_row(r, carry):
        for c in range(g.tiles):
            mm[r, :, lane(c)] = flat[pl.ds(c * block + r, g.sub, stride=g.rows), :]
        return carry

    lax.fori_loop(0, g.rows, one_row, 0, unroll=2)
    top = top_half(g)
    for out, start in ((up, g.rows - g.halo), (down, 0)):
        for c in range(g.tiles):
            for i in range(g.halo // 2):
                out[i, :, lane(c)] = jnp.where(
                    top, mm[start + 2 * i, :, lane(c)], mm[start + 2 * i + 1, :, lane(c)])


def unpack_pair(g, top, value):
    other = swap_halves(g, value)
    return jnp.where(top, value, other), jnp.where(top, other, value)


def signed_coriolis(g, c):
    column = (lax.broadcasted_iota(jnp.int32, (g.sub, LANES), 1) + c * LANES).astype(jnp.float32)
    f = 0.5 + column / g.columns
    return jnp.where(top_half(g), f, -f)


def over_rows(low, high, one_row):
    assert (high - low) % 2 == 0

    def turn(i, carry):
        one_row(low + 2 * i)
        one_row(low + 2 * i + 1)
        return carry

    lax.fori_loop(0, (high - low) // 2, turn, 0)


def advance(g, low, high, scale, uv, uv0, coefs, mass=None, tracer=None):
    top = top_half(g)
    carry_rows, turn_rows, shrink_rows, inverse_rows = coefs

    def put(target, e, c, value):
        if target is None:
            return
        if callable(target):
            target(e, c, value)
        else:
            target[e, :, lane(c)] = value

    def one_row(e):
        here = row_of(g, uv, e)
        if mass is not None:
            flux, hh0, uv_out, hh_out, flux_out = mass
            uv_columns = column_differences(g, here, False)
            flux_columns = column_differences(g, row_of(g, flux, e), False)
        if tracer is not None:
            qq, qq0, qq_out = tracer
            qq_columns = column_differences(g, row_of(g, qq, e), False)
        for c in range(g.tiles):
            swapped = swap_halves(g, here[c])
            east = jnp.where(top, here[c], swapped)
            north = jnp.where(top, swapped, here[c])
            along = carry_rows[e, :, lane(c)] * scale
            if tracer is not None:
                rows = qq[e + 1, :, lane(c)] - qq[e - 1, :, lane(c)]
                put(qq_out, e, c, qq0[e, :, lane(c)]
                    + along * (east * rows + north * qq_columns[c]))
            if mass is not None:
                rows = uv[e + 1, :, lane(c)] - uv[e - 1, :, lane(c)]
                uv_new = (uv0[e, :, lane(c)] + along * (east * rows + north * uv_columns[c])
                          + (turn_rows[e, :, lane(c)] * scale) * swapped)
                put(uv_out, e, c, uv_new)
                rows = flux[e + 1, :, lane(c)] - flux[e - 1, :, lane(c)]
                mixed = jnp.where(top, rows, flux_columns[c])
                hh_new = hh0[e, :, lane(c)] + (shrink_rows[e, :, lane(c)] * scale) * (
                    mixed + swap_halves(g, mixed))
                put(hh_out, e, c, hh_new)
                if flux_out is not None:
                    put(flux_out, e, c, hh_new * uv_new * inverse_rows[e, :, lane(c)])

    over_rows(low, high, one_row)


def fill_flux(g, low, high, uv, hh, inverse, flux):
    def one_row(e):
        for c in range(g.tiles):
            flux[e, :, lane(c)] = (
                hh[e, :, lane(c)] * uv[e, :, lane(c)] * inverse[e, :, lane(c)])

    over_rows(low, high, one_row)


def add_gradient(g, low, high, scale, mm, uv, hh, coefs, uv_out, pull, flux_out):
    top = top_half(g)
    carry_rows, turn_rows, shrink_rows, inverse_rows = coefs

    def one_row(e):
        columns = column_differences(g, row_of(g, mm, e), True)
        for c in range(g.tiles):
            gradient = jnp.where(
                top, mm[e + 1, :, lane(c)] - mm[e - 1, :, lane(c)], columns[c])
            force = carry_rows[e, :, lane(c)] * gradient
            value = uv[e, :, lane(c)] + scale * force
            uv_out[e, :, lane(c)] = value
            pull[e, :, lane(c)] = force
            flux_out[e, :, lane(c)] = (
                hh[e, :, lane(c)] * value * inverse_rows[e, :, lane(c)])

    over_rows(low, high, one_row)


def prepare_kernel(g, place, uv_own, hh_own, up, down, metric, active,
                   uv0, hh0, carry, turn, shrink, inverse, uv1, hh1,
                   flux, s_metric, s_active, sem):
    n = g.halo
    w = g.wide
    own = pl.ds(n, g.rows)
    copies = [
        pltpu.make_async_copy(uv_own, uv0.at[own], sem.at[0]),
        pltpu.make_async_copy(hh_own, hh0.at[own], sem.at[1]),
    ]
    for one in copies:
        one.start()
    top = top_half(g)
    low, high = pl.ds(0, g.margin), pl.ds(g.margin + g.rows, g.margin)
    own = pl.ds(g.margin, g.rows)
    m = n + n // 2
    for c in range(g.tiles):
        for span, value, count in (
            (low, up[m, :, lane(c)], up[m + 1, :, lane(c)]),
            (own, metric[:, lane(c)], active[:, lane(c)]),
            (high, down[m, :, lane(c)], down[m + 1, :, lane(c)]),
        ):
            s_metric[c, span] = value
            s_active[c, span] = count
    for halo, start in ((up, 0), (down, n + g.rows)):
        for c in range(g.tiles):
            for i in range(n):
                uv0[start + i, :, lane(c)] = halo[i, :, lane(c)]
            for i in range(n // 2):
                one, two = unpack_pair(g, top, halo[n + i, :, lane(c)])
                hh0[start + 2 * i, :, lane(c)] = one
                hh0[start + 2 * i + 1, :, lane(c)] = two
    layer = (place[0] * g.layers + lax.rem(sublane_index(g), g.layers)).astype(jnp.float32)
    metric_rows = s_metric.reshape(g.tiles * g.plane, LANES)
    active_rows = s_active.reshape(g.tiles * g.plane, LANES)
    shift = g.margin - n
    coriolis = [signed_coriolis(g, c) for c in range(g.tiles)]
    for one in copies:
        one.wait()

    def one_row(e):
        for c in range(g.tiles):
            value = spread(metric_rows, g.plane, c, e + shift)
            live = layer < spread(active_rows, g.plane, c, e + shift)
            along = jnp.where(live, -0.5 * value, 0.0)
            carry[e, :, lane(c)] = along
            shrink[e, :, lane(c)] = along * value
            turn[e, :, lane(c)] = jnp.where(live, coriolis[c], 0.0)
            one_over = 1.0 / value
            inverse[e, :, lane(c)] = one_over
            flux[e, :, lane(c)] = hh0[e, :, lane(c)] * uv0[e, :, lane(c)] * one_over

    over_rows(0, w, one_row)
    advance(g, 1, w - 1, time_step * FRACTIONS[0], uv0, uv0, (carry, turn, shrink, inverse),
            mass=(flux, hh0, uv1, hh1, None))


def with_pull(g, uv0, pull, scale):
    class Sum:
        def __getitem__(self, where):
            return uv0[where] + pull[where] * scale

    return Sum()


def first_kernel(g, uv0, hh0, carry, turn, shrink, inverse, uv1_part, hh1, mm_own, m_up, m_down,
                 uv1, uv2, uv3, hh3, sizes, mm, pull, flux0, flux1, sem):
    n = g.halo
    w = g.wide
    coefs = (carry, turn, shrink, inverse)
    copy = pltpu.make_async_copy(mm_own, mm.at[pl.ds(n, g.rows)], sem.at[0])
    copy.start()
    top = top_half(g)
    for halo, start in ((m_up, 0), (m_down, n + g.rows)):
        for c in range(g.tiles):
            for i in range(n // 2):
                one, two = unpack_pair(g, top, halo[i, :, lane(c)])
                mm[start + 2 * i, :, lane(c)] = one
                mm[start + 2 * i + 1, :, lane(c)] = two
    copy.wait()
    s = [time_step * fraction for fraction in FRACTIONS]
    add_gradient(g, 1, w - 1, s[0], mm, uv1_part, hh1, coefs, uv1, pull, flux1)
    advance(g, 2, w - 2, s[1], uv1, with_pull(g, uv0, pull, s[1]), coefs,
            mass=(flux1, hh0, uv2, None, flux0))
    advance(g, 3, w - 3, s[2], uv2, with_pull(g, uv0, pull, s[2]), coefs,
            mass=(flux0, hh0, uv3, hh3, None))
    first = len(FRACTIONS)
    for i in range((w - 2 * first) // 2):
        e = first + 2 * i
        for c in range(g.tiles):
            sizes[i, :, lane(c)] = jnp.abs(
                jnp.where(top, hh3[e, :, lane(c)], hh3[e + 1, :, lane(c)]))


def any_lane(c):
    return pl.ds(pl.multiple_of(c * LANES, LANES), LANES)


def suffix_sums(g, layer, value):
    value = value + jnp.where(layer < g.layers - 1, pltpu.roll(value, g.sub - 1, 0), 0.0)
    return value + jnp.where(layer < g.layers - 2, pltpu.roll(value, g.sub - 2, 0), 0.0)


def prefix_sums(g, layer, value):
    value = value + jnp.where(layer >= 1, pltpu.roll(value, 1, 0), 0.0)
    return value + jnp.where(layer >= 2, pltpu.roll(value, 2, 0), 0.0)


def place_rows(g, rows, place_in, j, value):
    rows = jnp.where(place_in == j, pltpu.roll(value, j, 0) if j else value, rows)
    return jnp.where(place_in == j + 1, pltpu.roll(value, (j + 1 - g.layers) % g.sub, 0), rows)


def second_mass_kernel(g, own, other, total):
    place_in = sublane_index(g)
    layer = lax.rem(place_in, g.layers)
    pairs = own.shape[0]

    def one_tile(c, carry):
        for start in range(0, total.shape[0], g.sub):
            rows = jnp.zeros((g.sub, LANES), jnp.float32)
            for j in range(0, g.sub, 2):
                i = (start + j) // 2
                if i < pairs:
                    value = own[i, :, any_lane(c)] + other[i, :, any_lane(c)]
                    rows = place_rows(g, rows, place_in, j, suffix_sums(g, layer, value))
            total[pl.ds(start, g.sub), any_lane(c)] = rows
        return carry

    lax.fori_loop(0, g.tiles, one_tile, 0)


def spread_total(g, layer, prefix):
    value = jnp.where(layer == g.layers - 1, prefix, 0.0)
    value = value + jnp.where(layer < g.layers - 1, pltpu.roll(value, g.sub - 1, 0), 0.0)
    return value + jnp.where(layer < g.layers - 2, pltpu.roll(value, g.sub - 2, 0), 0.0)


def spread_first(g, layer, suffix):
    value = jnp.where(layer == 0, suffix, 0.0)
    value = value + jnp.where(layer == 1, pltpu.roll(value, 1, 0), 0.0)
    return value + jnp.where(layer >= 2, pltpu.roll(value, 2, 0), 0.0)


def second_exner_kernel(g, place, jumps, own, other, above, weighted, chip_sum, s_above):
    me = place[0]
    partner = me + 1 - 2 * lax.rem(me, 2)
    low_chip, high_chip, low_group, high_group = switches(me)
    height = s_above.shape[1]
    for c in range(g.tiles):
        s_above[c] = above[:, lane(c)] * low_chip
    flat = s_above.reshape(g.tiles * height, LANES)
    place_in = sublane_index(g)
    layer = lax.rem(place_in, g.layers)
    top = top_half(g)

    def jump_of(owner):
        value = jumps[owner * g.layers]
        for k in range(1, g.layers):
            value = jnp.where(layer == k, jumps[owner * g.layers + k], value)
        return value

    my_jump, their_jump = jump_of(me), jump_of(partner)
    pairs = own.shape[0]

    def terms(prefix, jump):
        pressure = top_pressure + prefix * (1.0 / g.levels)
        return suffix_sums(g, layer, jump * jnp.exp(exner_power * jnp.log(pressure)))

    def one_tile(c, carry):
        for start in range(0, height, g.sub):
            rows = jnp.zeros((g.sub, LANES), jnp.float32)
            for j in range(0, g.sub, 2):
                i = (start + j) // 2
                if i >= pairs:
                    continue
                mine = prefix_sums(g, layer, own[i, :, any_lane(c)])
                theirs = prefix_sums(g, layer, other[i, :, any_lane(c)])
                outer = jnp.where(top, spread(flat, height, c, 2 * i),
                                  spread(flat, height, c, 2 * i + 1))
                my_terms = terms(
                    mine + outer + spread_total(g, layer, theirs) * low_group, my_jump)
                their_terms = terms(
                    theirs + outer + spread_total(g, layer, mine) * high_group, their_jump)
                weighted[i, :, any_lane(c)] = (
                    my_terms + spread_first(g, layer, their_terms) * high_group)
                rows = place_rows(g, rows, place_in, j, my_terms + their_terms)
            chip_sum[pl.ds(start, g.sub), any_lane(c)] = rows
        return carry

    lax.fori_loop(0, g.tiles, one_tile, 0)


def tracer_kernel(g, late_up, late_down, qq_own, uv0, uv1, uv2, carry, qq3, qq0, qq1, qq2, sem):
    n = g.halo
    w = g.wide
    copy = pltpu.make_async_copy(qq_own, qq0.at[pl.ds(n, g.rows)], sem.at[0])
    copy.start()
    for halo, start in ((late_up, 0), (late_down, n + g.rows)):
        for c in range(g.tiles):
            for i in range(n):
                qq0[start + i, :, lane(c)] = halo[i, :, lane(c)]
    copy.wait()
    s = [time_step * fraction for fraction in FRACTIONS]
    coefs = (carry, None, None, None)
    advance(g, 1, w - 1, s[0], uv0, None, coefs, tracer=(qq0, qq0, qq1))
    advance(g, 2, w - 2, s[1], uv1, None, coefs, tracer=(qq1, qq0, qq2))
    advance(g, 3, w - 3, s[2], uv2, None, coefs, tracer=(qq2, qq0, qq3))


def again_kernel(g, uv3, hh3, carry, turn, shrink, inverse, uv4, hh4, flux):
    first = len(FRACTIONS)
    w = g.wide
    fill_flux(g, first, w - first, uv3, hh3, inverse, flux)
    advance(g, first + 1, w - first - 1, time_step * FRACTIONS[0], uv3, uv3,
            (carry, turn, shrink, inverse), mass=(flux, hh3, uv4, hh4, None))


def last_kernel(g, place, weighted, beneath, geopot, late_up, late_down,
                uv3, hh3, qq3, carry, turn, shrink, inverse, uv4_part, hh4,
                u_out, v_out, h_out, q1_out, q2_out,
                mm, pull, uv4, uv5, flux0, flux1, qq4, qq5, s_geopot, s_beneath,
                s_uv, s_hh, s_qq, sem):
    n = g.halo
    first = len(FRACTIONS)
    w = g.wide
    s = [time_step * fraction for fraction in FRACTIONS]
    coefs = (carry, turn, shrink, inverse)
    top = top_half(g)
    high_chip = switches(place[0])[1]
    height = s_beneath.shape[1]
    for c in range(g.tiles):
        s_geopot[c, pl.ds(0, g.margin)] = late_up[n, :, lane(c)]
        s_geopot[c, pl.ds(g.margin, g.rows)] = geopot[:, lane(c)]
        s_geopot[c, pl.ds(g.margin + g.rows, g.margin)] = late_down[n, :, lane(c)]
        s_beneath[c] = beneath[:, lane(c)] * high_chip
    geopot_rows = s_geopot.reshape(g.tiles * g.plane, LANES)
    beneath_rows = s_beneath.reshape(g.tiles * height, LANES)
    shift = g.margin - n

    def one_pair(i, carried):
        e = first + 2 * i
        for c in range(g.tiles):
            base = jnp.where(top, spread(geopot_rows, g.plane, c, e + shift),
                             spread(geopot_rows, g.plane, c, e + 1 + shift))
            offset = jnp.where(top, spread(beneath_rows, height, c, 2 * i),
                               spread(beneath_rows, height, c, 2 * i + 1))
            one, two = unpack_pair(g, top, base + (weighted[i, :, lane(c)] + offset))
            mm[e, :, lane(c)] = one
            mm[e + 1, :, lane(c)] = two
        return carried

    lax.fori_loop(0, (w - 2 * first) // 2, one_pair, 0)
    add_gradient(g, first + 1, w - first - 1, s[0], mm, uv4_part, hh4, coefs, uv4, pull, flux1)
    advance(g, 4, w - 4, s[0], uv3, None, coefs, tracer=(qq3, qq3, qq4))
    advance(g, 5, w - 5, s[1], uv4, with_pull(g, uv3, pull, s[1]), coefs,
            mass=(flux1, hh3, uv5, None, flux0), tracer=(qq4, qq3, qq5))
    block = g.sub * g.rows

    def store_in(scratch):
        flat = scratch.reshape(g.tiles * block, LANES)

        def store(e, c, value):
            flat[pl.ds(c * block + e - n, g.sub, stride=g.rows), :] = value

        return store

    advance(g, 6, w - 6, s[2], uv5, with_pull(g, uv3, pull, s[2]), coefs,
            mass=(flux0, hh3, store_in(s_uv), store_in(s_hh), None),
            tracer=(qq5, qq3, store_in(s_qq)))
    copies = []
    for target, scratch, slot in ((u_out, s_uv, 0), (v_out, s_uv, 1), (h_out, s_hh, 0),
                                  (q1_out, s_qq, 0), (q2_out, s_qq, 1)):
        for c in range(g.tiles):
            copies.append(pltpu.make_async_copy(
                scratch.at[c, slot], target.at[:, :, lane(c)], sem.at[0]))
    for one in copies:
        one.start()
    for one in copies:
        one.wait()


def local(
    wind_east,
    wind_north,
    thickness,
    tracer_one,
    tracer_two,
    theta_step,
    surface_geopot,
    map_factor,
    active_layers,
):
    layers, rows, columns = thickness.shape
    groups = lax.axis_size("lev")
    assert groups == 4
    g = Geometry(layers, rows, columns, layers * groups)
    n, w = g.halo, g.wide
    first = len(FRACTIONS)
    pairs = (w - 2 * first) // 2
    height = -(-2 * pairs // 8) * 8
    count = lax.axis_size("row")
    forward = [(i, (i + 1) % count) for i in range(count)]
    backward = [(i, (i - 1) % count) for i in range(count)]
    on_chip = [(i, i ^ 1) for i in range(groups)]
    over_chips = [(i, i ^ 2) for i in range(groups)]
    place = lax.axis_index("lev").astype(jnp.int32).reshape(1)

    def shape(*dims):
        return pltpu.VMEM(dims, jnp.float32)

    def move(value, axis, pairs_of):
        return pltpu.with_memory_space_constraint(
            lax.ppermute(value, axis, pairs_of), pltpu.VMEM)

    def call(body, outs, ins, scratch, name, out_specs=None):
        return pl.pallas_call(
            functools.partial(body, g),
            out_shape=outs,
            in_specs=ins,
            out_specs=out_specs if out_specs is not None else [VMEM] * len(outs),
            scratch_shapes=scratch,
            compiler_params=pltpu.CompilerParams(vmem_limit_bytes=SCOPED_BYTES),
            name=name,
        )

    slab = shape(rows, g.sub, columns)
    broad = shape(w, g.sub, columns)
    flat = shape(rows, columns)
    plane_out = shape(height, columns)
    stack = shape(pairs, g.sub, columns)
    fields = pltpu.VMEM((g.tiles, 2, layers, rows, LANES), jnp.float32)
    plane = pltpu.VMEM((g.tiles, g.plane, LANES), jnp.float32)
    offsets = pltpu.VMEM((g.tiles, height, LANES), jnp.float32)
    dma = pltpu.SemaphoreType.DMA
    early = n + n // 2 + 2

    other_h = move(thickness, "lev", on_chip)
    (up, down, late_up, late_down, uv, hh, qq, mass, metric, active, jumps) = call(
        pack_kernel,
        [shape(early, g.sub, columns)] * 2 + [shape(n + 1, g.sub, columns)] * 2
        + [slab] * 3 + [flat] * 3 + [shape(g.levels, g.sub, LANES)],
        [FAR] * 9,
        [fields] * 3 + [pltpu.VMEM((rows, columns), jnp.int32), flat,
                        pltpu.SMEM((g.levels,), jnp.float32), dma((3,))],
        "pack",
    )(*(pltpu.with_memory_space_constraint(value, pltpu.HBM) for value in (
        wind_east, wind_north, thickness, tracer_one, tracer_two,
        map_factor, active_layers, surface_geopot, theta_step)))
    (total,) = call(chip_mass_kernel, [flat], [VMEM] * 2, [], "chip_mass")(mass, other_h)
    up_in = move(up, "row", forward)
    down_in = move(down, "row", backward)
    weighted, chip_sum = call(
        exner_kernel, [shape(layers, rows, columns), flat], [SMEM] + [VMEM] * 4, [], "exner",
    )(place, jumps, thickness, other_h, move(total, "lev", over_chips))
    m_up, m_down, mm = call(
        montgomery_kernel, [shape(n // 2, g.sub, columns)] * 2 + [slab],
        [SMEM] + [VMEM] * 3, [fields], "montgomery",
    )(place, weighted, move(chip_sum, "lev", over_chips), surface_geopot)
    m_up_in = move(m_up, "row", forward)
    m_down_in = move(m_down, "row", backward)
    uv0, hh0, carry, turn, shrink, inverse, uv1_part, hh1 = call(
        prepare_kernel, [broad] * 8, [SMEM] + [VMEM] * 6,
        [broad] + [plane] * 2 + [dma((2,))], "prepare",
    )(place, uv, hh, up_in, down_in, metric, active)
    uv1, uv2, uv3, hh3, sizes = call(
        first_kernel, [broad] * 4 + [stack], [VMEM] * 11, [broad] * 4 + [dma((1,))], "first",
    )(uv0, hh0, carry, turn, shrink, inverse, uv1_part, hh1, mm, m_up_in, m_down_in)
    late_up_in = move(late_up, "row", forward)
    late_down_in = move(late_down, "row", backward)
    other_sizes = move(sizes, "lev", on_chip)
    (total,) = call(second_mass_kernel, [plane_out], [VMEM] * 2, [], "second_mass")(
        sizes, other_sizes)
    uv4_part, hh4 = call(again_kernel, [broad] * 2, [VMEM] * 6, [broad], "again")(
        uv3, hh3, carry, turn, shrink, inverse)
    weighted, chip_sum = call(
        second_exner_kernel, [stack, plane_out], [SMEM] + [VMEM] * 4, [offsets], "second_exner",
    )(place, jumps, sizes, other_sizes, move(total, "lev", over_chips))
    (qq3,) = call(
        tracer_kernel, [broad], [VMEM] * 7, [broad] * 3 + [dma((1,))], "tracer",
    )(late_up_in, late_down_in, qq, uv0, uv1, uv2, carry)
    return tuple(call(
        last_kernel, [jax.ShapeDtypeStruct((layers, rows, columns), jnp.float32)] * 5,
        [SMEM] + [VMEM] * 14,
        [broad] * 8 + [plane, offsets] + [fields] * 3 + [dma((1,))],
        "last", [FAR] * 5,
    )(place, weighted, move(chip_sum, "lev", over_chips), surface_geopot, late_up_in,
      late_down_in, uv3, hh3, qq3, carry, turn, shrink, inverse, uv4_part, hh4))


def solution(mesh):
    state = P("lev", "row", None)
    flat = P("row", None)
    return jax.shard_map(
        local,
        mesh=mesh,
        in_specs=(state,) * 5 + (P(), flat, flat, flat),
        out_specs=(state,) * 5,
        check_vma=False,
    )
```
